256 devices in a mesh: seq: 64 (over y, z, core), section: 4 (over x).
Axes of the slice: x: 4, y: 4, z: 8, core: 2. Of those that a mesh axis runs over, the one named last changes fastest.
Arguments:
- acts: bfloat16 [16384, 1408], P('seq'), may hold values from -16 to 16
- pre_act: bfloat16 [16384, 1536], P('seq', 'section'), may hold values from -6 to 6
- emb_grad: bfloat16 [8192, 1536], P('seq', 'section'), may hold values from -6 to 6
- filters: bfloat16 [7040, 1536], P('seq', 'section'), may hold values from -0.0625 to 0.0625
Outputs:
- input_grad: bfloat16 [16384, 1408], P('seq', 'section')
- filter_grad: float32 [7040, 1536], P('seq', 'section')
The draws below stay inside these ranges and needn't reach their ends.
All inputs are finite; a program needn't handle non-finite values.
Results may differ from the reference program's by a relative error of at most 0.0049.
Values may be sent and summed in bfloat16 or wider, within the bound.
A program may use at most 128 MiB of HBM per device.

```python
import jax
import jax.numpy as jnp
from jax import lax

C_IN = 1408
C_OUT = 1536
KERNEL = 5
SEQS = 1
ROWS = 16384
LENGTH = 16384
EMB_ROWS = 8192


def spiked(result, own_key, source, target, blocks, factor):
    owner, partner = [(jnp.arange(result.shape[position]) // (result.shape[position] // blocks)).reshape([-1 if axis == position else 1 for axis in range(result.ndim)]) for position in (source, target)]
    chosen = jax.random.permutation(own_key, blocks)[partner]
    strong = (owner == chosen) | (owner == (partner + blocks // 2) % blocks)
    return jnp.where(strong, factor * result, result)


def shard_levels(rng, extent, cuts, low, top_value):
    def one(dim, shards_of):
        draws = jax.random.uniform(jax.random.fold_in(jax.random.fold_in(rng, 6), dim), (shards_of,), jnp.float32, low / len(cuts), top_value / len(cuts))
        return jnp.repeat(jnp.exp(draws), extent[dim] // shards_of).reshape((-1,) + (1,) * (len(extent) - dim - 1))

    level = one(*cuts[0])
    for cut in cuts[1:]:
        level = level * one(*cut)
    return level


def scatter_about(rng, extent, spread, limit, shards=(), dtype=jnp.bfloat16):
    values = spread * jax.random.normal(rng, extent, jnp.float32)
    if shards:
        values = values * shard_levels(rng, extent, shards, -0.22, 0.18)
    return jnp.clip(values, -limit, limit).astype(dtype)


def bell_draw_with(key, shape, spread, reach, cuts, heavy, dtype=jnp.bfloat16):
    entries = spread * jax.random.normal(key, shape, jnp.float32)
    if cuts:
        entries = entries * shard_levels(key, shape, cuts, -0.22, 0.18)
    return jnp.clip(spiked(entries, jax.random.fold_in(key, 3), *heavy), -reach, reach).astype(dtype)


def setup_inputs(seed: int = 0) -> dict:
    seeds = jax.random.split(jax.random.key(seed), 5)
    acts = bell_draw_with(seeds[0], (ROWS, C_IN), 1.0, 16.0, ((0, 64),), (0, 1, 64, 4.0))
    pre_act = scatter_about(seeds[1], (ROWS, C_OUT), 1.5, 6.0, ((0, 64), (1, 4)))
    emb_grad = scatter_about(seeds[2], (EMB_ROWS, C_OUT), 1.0, 6.0, ((0, 64), (1, 4)))
    filters = scatter_about(seeds[3], (KERNEL * C_IN, C_OUT), (KERNEL * C_IN) ** -0.5, 0.0625, ((0, 64), (1, 4)))
    return dict(acts=acts, pre_act=pre_act, emb_grad=emb_grad, filters=filters)


def gelu_slope(value):
    cumul = 0.5 * (1.0 + lax.erf(value * 0.7071067811865476))
    dens = jnp.exp(-0.5 * value * value) * 0.3989422804014327
    return cumul + value * dens

def reference(acts, pre_act, emb_grad, filters):
    upward = jnp.repeat(emb_grad.astype(jnp.float32), 2, axis=0) * 0.5
    zvalue = pre_act.astype(jnp.float32)
    dz_grad = (upward * gelu_slope(zvalue)).astype(jnp.bfloat16)
    act_pad = jnp.pad(acts.reshape(SEQS, LENGTH, C_IN), ((0, 0), (2, 2), (0, 0)))
    grad_pad = jnp.pad(dz_grad.reshape(SEQS, LENGTH, C_OUT), ((0, 0), (2, 2), (0, 0)))
    taps_w = filters.reshape(KERNEL, C_IN, C_OUT)
    pieces = []
    input_acc = jnp.zeros((ROWS, C_IN), jnp.float32)
    for k in range(KERNEL):
        window = act_pad[:, k:k + LENGTH].reshape(ROWS, C_IN)
        pieces.append(jnp.dot(window.T, dz_grad, preferred_element_type=jnp.float32))
        shifted = grad_pad[:, 4 - k:4 - k + LENGTH].reshape(ROWS, C_OUT)
        input_acc = input_acc + jnp.dot(shifted, taps_w[k].T, preferred_element_type=jnp.float32)
    scale_value = jnp.float32(1.0) / jnp.sqrt(jnp.float32(ROWS))
    filter_grad = jnp.concatenate(pieces, axis=0) * scale_value
    return (input_acc.astype(jnp.bfloat16), filter_grad)
```

```python
import functools
import math

import jax
import jax.numpy as jnp
from jax import lax
from jax.experimental import pallas as pl
from jax.experimental.pallas import tpu as pltpu
from jax.sharding import PartitionSpec as P

MESH = pl.DeviceIdType.MESH
F32, BF16 = jnp.float32, jnp.bfloat16
TAPS = 5
NY, NZ, NX = 4, 8, 4
SHARDS = 64
C_IN = 1408
ROWS = 256
PART = 384
OWN = 110
PAD = 112
SLOT = 128
SLICE = C_IN // NX
SPAN = C_IN + 256


def gelu_slope(value):
    cumul = 0.5 * (1.0 + lax.erf(value * 0.7071067811865476))
    dens = jnp.exp(-0.5 * value * value) * 0.3989422804014327
    return cumul + value * dens


def nt_dot(a, b):
    return lax.dot_general(a, b, (((1,), (1,)), ((), ())), preferred_element_type=F32)


def wrap(value, size):
    return lax.rem(value + 2 * size, size)


def kernel(scale, acts, pre, emb, filt, ig_out, fg_out, slots, packed, window, rim, dz, part, send_r, send_l, recv_r, recv_l,
           small_sr, small_sl, small_rr, small_rl, halo_s, halo_r, ig_own, ig_s, ig_r, sems, gather_sem, sib_sem, red_sem, x_sem):
    s = lax.axis_index("seq")
    x = lax.axis_index("section")
    y, z, h = s // 16, lax.rem(s, 16) // 2, lax.rem(s, 2)

    def at(yy, zz, hh):
        return (wrap(yy, NY) * 16 + wrap(zz, NZ) * 2 + hh, x)

    sibling = (s + 1 - 2 * h, x)
    after = (lax.rem(s + 1, SHARDS), x)
    before = (lax.rem(s + SHARDS - 1, SHARDS), x)
    pending = []

    def send(src, dst, ssem, rsem, to):
        copy = pltpu.make_async_remote_copy(src_ref=src, dst_ref=dst, send_sem=ssem, recv_sem=rsem, device_id=to, device_id_type=MESH)
        copy.start()
        return copy

    def arrive(dst, rsem):
        pltpu.make_async_remote_copy(src_ref=dst, dst_ref=dst, send_sem=rsem, recv_sem=rsem, device_id=sibling, device_id_type=MESH).wait_recv()

    here = pl.ds(pl.multiple_of(h * ROWS, ROWS), ROWS)
    load_acts = pltpu.make_async_copy(acts, window.at[here, pl.ds(0, C_IN)], sems.at[0])
    load_acts.start()

    block = jnp.concatenate([filt[...].astype(F32), jnp.zeros((SLOT - OWN, PART), F32)], axis=0)
    shift = lax.rem(s * OWN, 16)
    slots[h, y, z] = pltpu.roll(block, shift, 0).astype(BF16)

    barrier = pltpu.get_barrier_semaphore()
    cross = (jnp.where(h == 0, before[0], after[0]), x)
    peers = [at(y + 1, z, h), at(y - 1, z, h), at(y, z + 1, h), at(y, z - 1, h), sibling, cross]
    peers += [(s, lax.rem(x + i, NX)) for i in range(1, NX)]
    for peer in peers:
        pl.semaphore_signal(barrier, inc=1, device_id=peer, device_id_type=MESH)
    pl.semaphore_wait(barrier, len(peers))

    def make_dz():
        pick = (lax.broadcasted_iota(jnp.int32, (ROWS, ROWS // 2), 0) // 2
                == lax.broadcasted_iota(jnp.int32, (ROWS, ROWS // 2), 1)).astype(BF16)
        up = jnp.dot(pick, emb[...], preferred_element_type=F32) * 0.5
        rim[8:8 + ROWS, :] = (up * gelu_slope(pre[...].astype(F32))).astype(BF16).astype(F32)
        halo_s[0] = rim[8:24, :].astype(BF16)
        halo_s[1] = rim[8 + ROWS - 16:8 + ROWS, :].astype(BF16)

    def send_halo():
        pending.append(send(halo_s.at[0], halo_r.at[0], sems.at[1], sems.at[3], before))
        pending.append(send(halo_s.at[1], halo_r.at[1], sems.at[2], sems.at[4], after))

    def make_taps():
        arrive(halo_r.at[0], sems.at[3])
        arrive(halo_r.at[1], sems.at[4])
        low = jnp.where(s > 0, 1.0, 0.0)
        high = jnp.where(s < SHARDS - 1, 1.0, 0.0)
        rim[0:8, :] = halo_r[1].astype(F32)[8:16] * low
        rim[8 + ROWS:16 + ROWS, :] = halo_r[0].astype(F32)[0:8] * high
        for k in range(TAPS):
            dz[k, here, :] = rim[10 - k:10 - k + ROWS, :].astype(BF16)
        pending.append(send(dz.at[:, here], dz.at[:, here], sems.at[5], sems.at[6], sibling))

    def send_acts():
        load_acts.wait()
        lanes = window.at[here, pl.ds(0, C_IN)]
        pending.append(send(lanes, lanes, sems.at[7], sems.at[8], sibling))

    def sibling_inputs():
        there = pl.ds(pl.multiple_of((1 - h) * ROWS, ROWS), ROWS)
        arrive(window.at[there, pl.ds(0, C_IN)], sems.at[8])
        arrive(dz.at[:, there], sems.at[6])
        window[:, C_IN:SPAN] = window[:, 0:SPAN - C_IN]

    def partial(yy, zz):
        owner = yy * 16 + zz * 2 + h
        start = owner * OWN
        tap = start // C_IN
        column = start - tap * C_IN
        tile = column // 128
        off = column - tile * 128
        rest = C_IN - column
        row = lax.broadcasted_iota(jnp.int32, (PAD, 256), 0)
        lane = lax.broadcasted_iota(jnp.int32, (PAD, 256), 1)
        seen = window[:, pl.ds(pl.multiple_of(tile * 128, 128), 256)]
        hit = (lane - row == off) & (row < jnp.minimum(OWN, rest))
        chosen = nt_dot(jnp.where(hit, 1.0, 0.0).astype(BF16), seen).astype(BF16)
        part[yy, zz] = jnp.dot(chosen, dz[tap], preferred_element_type=F32)

        @pl.when(rest < OWN)
        def _():
            hit2 = (lane - row == off) & (row >= rest) & (row < OWN)
            chosen2 = nt_dot(jnp.where(hit2, 1.0, 0.0).astype(BF16), seen).astype(BF16)
            part[yy, zz] += jnp.dot(chosen2, dz[lax.rem(tap + 1, TAPS)], preferred_element_type=F32)

    def pack():
        packed[0:16, :] = jnp.zeros((16, PART), BF16)

        def one(i, carry):
            for j in range(8):
                base = pl.multiple_of(i * (8 * OWN) + (j * OWN) // 16 * 16, 16)
                block = slots[j % 2, i // 2, lax.rem(i, 2) * 4 + j // 2]
                packed[pl.ds(base, 16), :] += block[0:16]
                packed[pl.ds(base + 16, SLOT - 16), :] = block[16:SLOT]
            return carry

        lax.fori_loop(0, SHARDS // 8, one, 0)

    def input_grad():
        def one(i, carry):
            dest = lax.rem(x + 1 + i, NX)
            total = jnp.zeros((SLICE, ROWS), F32)
            for k in range(TAPS):
                rows = packed[pl.ds(pl.multiple_of(k * C_IN + dest * SLICE, 16), SLICE), :]
                total += nt_dot(rows, dz[k, here, :])

            @pl.when(i < NX - 1)
            def _():
                ig_s[i] = total.astype(BF16)
                send(ig_s.at[i], ig_r.at[i], x_sem.at[0, i], x_sem.at[1, i], (s, dest))

            @pl.when(i == NX - 1)
            def _():
                ig_own[...] = total

            return carry

        lax.fori_loop(0, NX, one, 0)

    def finish_input_grad():
        total = ig_own[...]
        for i in range(NX - 1):
            arrive(ig_r.at[i], x_sem.at[1, i])
            total += ig_r[i].astype(F32)
        ig_out[...] = total.T.astype(BF16)
        for i in range(NX - 1):
            pltpu.make_async_remote_copy(src_ref=ig_s.at[i], dst_ref=ig_r.at[i], send_sem=x_sem.at[0, i], recv_sem=x_sem.at[1, i],
                                         device_id=sibling, device_id_type=MESH).wait_send()

    def ring(axis, step):
        return at(y + step, z, h) if axis == "y" else at(y, z + step, h)

    def run(hh, done):
        first, second = ("z", "y") if hh == 0 else ("y", "z")
        n1, n2 = (NZ, NY) if hh == 0 else (NY, NZ)
        p1, p2 = (z, y) if hh == 0 else (y, z)
        counts = {"g": 0, "sib": 0}
        waits = []

        def slab(a, b, lo=None, size=None):
            a = pl.ds(lo, size) if a is None else a
            return slots.at[hh, b, a] if hh == 0 else slots.at[hh, a, b]

        def push(ref, axis, step, sem):
            done.append(send(ref, ref, gather_sem.at[0, sem], gather_sem.at[1, sem], ring(axis, step)))

        def share(ref):
            i = counts["sib"]
            counts["sib"] += 1
            done.append(send(ref, ref, sib_sem.at[0, i], sib_sem.at[1, i], sibling))

        def g_first(t):
            if t == 0:
                ref = slab(p1, p2)
                push(ref, first, 1, 0)
                push(ref, first, -1, 4)
                share(ref)
                return
            ref = slab(wrap(p1 - t, n1), p2)
            arrive(ref, gather_sem.at[1, t - 1])
            if t < n1 // 2:
                push(ref, first, 1, t)
            share(ref)
            if t < n1 // 2:
                ref = slab(wrap(p1 + t, n1), p2)
                arrive(ref, gather_sem.at[1, 4 + t - 1])
                if t < n1 // 2 - 1:
                    push(ref, first, -1, 4 + t)
                share(ref)

        half = n1 // 2

        def g_second(t):
            if t == 0:
                ref = slab(None, p2, 0, n1)
                push(ref, second, 1, 8)
                push(ref, second, -1, 12)
                return
            last = t == n2 // 2
            right, left = wrap(p2 - t, n2), wrap(p2 + t, n2)
            a = slab(None, right, 0, half if last else n1)
            arrive(a, gather_sem.at[1, 8 + t - 1])
            if t == n2 // 2 - 1:
                push(slab(None, right, 0, half), second, 1, 8 + t)
            elif not last:
                push(a, second, 1, 8 + t)
            b = slab(None, left, half if last else 0, half if last else n1)
            arrive(b, gather_sem.at[1, 12 + t - 1])
            if t == n2 // 2 - 1:
                push(slab(None, left, half, half), second, -1, 12 + t)
            elif not last:
                push(b, second, -1, 12 + t)
            share(a)
            share(b)

        def g_sibling():
            o = 1 - hh
            m1, m2 = (NZ, NY) if o == 0 else (NY, NZ)
            q1, q2 = (z, y) if o == 0 else (y, z)

            def other(a, b, lo=None, size=None):
                a = pl.ds(lo, size) if a is None else a
                return slots.at[o, b, a] if o == 0 else slots.at[o, a, b]

            i = 0
            for t in range(m1 // 2 + 1):
                arrive(other(wrap(q1 - t, m1), q2), sib_sem.at[1, i])
                i += 1
                if 0 < t < m1 // 2:
                    arrive(other(wrap(q1 + t, m1), q2), sib_sem.at[1, i])
                    i += 1
            mid = m1 // 2
            for t in range(1, m2 // 2 + 1):
                last = t == m2 // 2
                arrive(other(None, wrap(q2 - t, m2), 0, mid if last else m1), sib_sem.at[1, i])
                arrive(other(None, wrap(q2 + t, m2), mid if last else 0, mid if last else m1), sib_sem.at[1, i + 1])
                i += 2

        heavy, light = second, first
        nb = n1

        def cell(i, d):
            return (d, i) if hh == 0 else (i, d)

        def compute(d):
            d = wrap(d, n2)

            def body(i, carry):
                for j in range(2):
                    partial(*cell(2 * i + j, d))
                return carry

            lax.fori_loop(0, nb // 2, body, 0)

        def base(t):
            return 0 if t == 0 else half + (t - 1) * nb

        top = n2 // 2

        def r_heavy(t):
            for side in range(2):
                out, got, sign = (send_r, recv_r, 1) if side == 0 else (send_l, recv_l, -1)
                d = wrap(p2 + sign * (top - t), n2)
                lo, size = ((0 if side == 0 else half), half) if t == 0 else (0, nb)
                if t > 0:
                    plo, psize = ((0 if side == 0 else half), half) if t == 1 else (0, nb)
                    arrive(got.at[pl.ds(base(t - 1), psize)], red_sem.at[1, side * 4 + t - 1])
                for i in range(size):
                    value = part[cell(lo + i, d)]
                    if t > 0 and plo <= lo + i < plo + psize:
                        value = value + got[base(t - 1) + lo + i - plo].astype(F32)
                    out[base(t) + i] = value.astype(BF16)
                span = pl.ds(base(t), size)
                done.append(send(out.at[span], got.at[span], red_sem.at[0, side * 4 + t], red_sem.at[1, side * 4 + t], ring(heavy, sign)))

        def r_heavy_end():
            for side in range(2):
                got = recv_r if side == 0 else recv_l
                plo, psize = ((0 if side == 0 else half), half) if top == 1 else (0, nb)
                arrive(got.at[pl.ds(base(top - 1), psize)], red_sem.at[1, side * 4 + top - 1])
            for i in range(nb):
                part[cell(i, p2)] += recv_r[base(top - 1) + i].astype(F32) + recv_l[base(top - 1) + i].astype(F32)

        ltop = n1 // 2

        def r_light(t):
            for side in range(2):
                if side == 1 and t == 0:
                    continue
                out, got, sign = (small_sr, small_rr, 1) if side == 0 else (small_sl, small_rl, -1)
                d = wrap(p1 + sign * (ltop - t), n1)
                value = part[cell(d, p2)]
                if t > (0 if side == 0 else 1):
                    arrive(got.at[t - 1], red_sem.at[1, 8 + side * 4 + t - 1])
                    value = value + got[t - 1].astype(F32)
                out[t] = value.astype(BF16)
                done.append(send(out.at[t], got.at[t], red_sem.at[0, 8 + side * 4 + t], red_sem.at[1, 8 + side * 4 + t], ring(light, sign)))

        def r_end():
            t = ltop - 1
            arrive(small_rr.at[t], red_sem.at[1, 8 + t])
            arrive(small_rl.at[t], red_sem.at[1, 12 + t])
            total = part[cell(p1, p2)] + small_rr[t].astype(F32) + small_rl[t].astype(F32)
            fg_out[...] = total[0:OWN] * scale

        def whole_input_grad():
            g_sibling()
            pack()
            input_grad()

        g_first(0)
        send_acts()
        make_dz()
        send_halo()
        g_first(1)
        make_taps()
        g_first(2)
        if hh == 1:
            g_second(0)
            sibling_inputs()
            compute(p2 + 4)
            r_heavy(0)
            compute(p2 + 3)
            compute(p2 - 3)
            g_second(1)
            r_heavy(1)
            compute(p2 + 2)
            compute(p2 - 2)
            g_second(2)
            r_heavy(2)
            compute(p2 + 1)
            compute(p2 - 1)
            compute(p2)
            g_second(3)
            r_heavy(3)
            g_second(4)
            whole_input_grad()
            r_heavy_end()
            r_light(0)
            r_light(1)
            r_end()
        else:
            sibling_inputs()
            compute(p2 + 2)
            r_heavy(0)
            g_first(3)
            compute(p2 + 1)
            compute(p2 - 1)
            g_first(4)
            g_second(0)
            r_heavy(1)
            compute(p2)
            g_second(1)
            r_heavy_end()
            r_light(0)
            g_second(2)
            r_light(1)
            r_light(2)
            r_light(3)
            whole_input_grad()
            r_end()
        finish_input_grad()
        for copy in done:
            copy.wait_send()

    for hh in range(2):
        @pl.when(h == hh)
        def _(hh=hh):
            pending.clear()
            run(hh, pending)


def shards(acts, pre_act, emb_grad, filters):
    total_rows = acts.shape[0] * lax.axis_size("seq")
    vmem = pl.BlockSpec(memory_space=pltpu.VMEM)
    return pl.pallas_call(
        functools.partial(kernel, 1.0 / math.sqrt(total_rows)),
        out_shape=(jax.ShapeDtypeStruct((ROWS, SLICE), BF16), jax.ShapeDtypeStruct((OWN, PART), F32)),
        in_specs=[pl.BlockSpec(memory_space=pl.ANY), vmem, vmem, vmem],
        out_specs=(vmem, vmem),
        scratch_shapes=[
            pltpu.VMEM((2, NY, NZ, SLOT, PART), BF16),
            pltpu.VMEM((TAPS * C_IN + 16, PART), BF16),
            pltpu.VMEM((2 * ROWS, SPAN), BF16),
            pltpu.VMEM((ROWS + 16, PART), F32),
            pltpu.VMEM((TAPS, 2 * ROWS, PART), BF16),
            pltpu.VMEM((NY, NZ, PAD, PART), F32),
            pltpu.VMEM((14, PAD, PART), BF16),
            pltpu.VMEM((14, PAD, PART), BF16),
            pltpu.VMEM((14, PAD, PART), BF16),
            pltpu.VMEM((14, PAD, PART), BF16),
            pltpu.VMEM((4, PAD, PART), BF16),
            pltpu.VMEM((4, PAD, PART), BF16),
            pltpu.VMEM((4, PAD, PART), BF16),
            pltpu.VMEM((4, PAD, PART), BF16),
            pltpu.VMEM((2, 16, PART), BF16),
            pltpu.VMEM((2, 16, PART), BF16),
            pltpu.VMEM((SLICE, ROWS), F32),
            pltpu.VMEM((NX - 1, SLICE, ROWS), BF16),
            pltpu.VMEM((NX - 1, SLICE, ROWS), BF16),
            pltpu.SemaphoreType.DMA((9,)),
            pltpu.SemaphoreType.DMA((2, 16)),
            pltpu.SemaphoreType.DMA((2, 16)),
            pltpu.SemaphoreType.DMA((2, 16)),
            pltpu.SemaphoreType.DMA((2, NX - 1)),
        ],
        compiler_params=pltpu.CompilerParams(collective_id=0, has_side_effects=True, vmem_limit_bytes=56 << 20),
    )(acts, pre_act, emb_grad, filters)


def solution(mesh):
    in_specs = (P("seq", None), P("seq", "section"), P("seq", "section"), P("seq", "section"))
    out_specs = (P("seq", "section"), P("seq", "section"))
    return jax.shard_map(shards, mesh=mesh, in_specs=in_specs, out_specs=out_specs, check_vma=False)
```

```python
import functools
import math

import jax
import jax.numpy as jnp
from jax import lax
from jax.experimental import pallas as pl
from jax.experimental.pallas import tpu as pltpu
from jax.sharding import PartitionSpec as P

MESH = pl.DeviceIdType.MESH
F32, BF16 = jnp.float32, jnp.bfloat16
I32 = jnp.int32
TAPS = 5
NX, NY, NZ = 4, 4, 8
GROUP = 8
SHARDS = 64
C_IN = 1408
ROWS = 256
PART = 384
OWN = 110
SLOT = 128
CHUNK = C_IN // GROUP
QUARTER = 48
SPACE = TAPS * CHUNK
SLICE = C_IN // NX
EDGE = 16


def gelu_slope(value):
    cumul = 0.5 * (1.0 + lax.erf(value * 0.7071067811865476))
    dens = jnp.exp(-0.5 * value * value) * 0.3989422804014327
    return cumul + value * dens


def nt_dot(a, b):
    return lax.dot_general(a, b, (((1,), (1,)), ((), ())), preferred_element_type=F32)


def iota(shape, axis):
    return lax.broadcasted_iota(I32, shape, axis)


def kernel(scale, acts, pre, emb, filt, ig_out, fg_out, f_out, f_in, f_slots, f_all, halo_p, halo_e, rim, dzx, dz, at_s, at, part,
           s_r, s_l, g_r, g_l, total_s, total_r, ig_own, ig_s, ig_r, fin_s, send_sem, recv_sem):
    s = lax.axis_index("seq")
    x = lax.axis_index("section")
    y, z, h = s // 16, lax.rem(s, 16) // 2, lax.rem(s, 2)
    j = 2 * y + h

    def at_place(yy, zz, hh):
        return lax.rem(yy + NY, NY) * 16 + lax.rem(zz + NZ, NZ) * 2 + hh

    def member(jj, zz):
        return (jj // 2) * 16 + zz * 2 + lax.rem(jj, 2)

    sibling = s + 1 - 2 * h
    after = lax.rem(s + 1, SHARDS)
    before = lax.rem(s + SHARDS - 1, SHARDS)

    def row_block(u):
        tile = (u * OWN) // 16 * 16
        chunk = (u * OWN) // CHUNK
        cut = (chunk + 1) * CHUNK - tile
        lead = u * OWN - tile
        return tile, chunk, cut, lead, cut < lead + OWN

    own_v, own_u = s // 8, lax.rem(s, 8)
    _, own_w, own_cut, own_lead, own_two = row_block(own_u)
    to_a = member(lax.rem(5 * own_v + own_w, GROUP), own_u)
    to_b = member(lax.rem(5 * own_v + own_w + 1, GROUP), own_u)
    my_tile, my_w, my_cut, my_lead, my_two = row_block(z)

    def tap_of(w):
        return lax.rem(2 * w + 3 * j, TAPS)

    def owner_of(w):
        return (8 * tap_of(w) + j) // 5 * 8 + z

    from_a, from_b = owner_of(my_w), owner_of(my_w + 1)

    ids = {}
    started = []

    def sem(name):
        return ids.setdefault(name, len(ids))

    def describe(name, src, dst, to):
        i = sem(name)
        return pltpu.make_async_remote_copy(src_ref=src, dst_ref=dst, send_sem=send_sem.at[i], recv_sem=recv_sem.at[i],
                                            device_id=to, device_id_type=MESH)

    def send(name, src, dst, to, when=None):
        copy = describe(name, src, dst, to)
        started.append((copy, when))
        if when is None:
            copy.start()
        else:
            pl.when(when)(copy.start)

    def arrive(name, dst, when=None):
        copy = describe(name, dst, dst, (sibling, x))
        if when is None:
            copy.wait_recv()
        else:
            pl.when(when)(copy.wait_recv)

    block = jnp.concatenate([filt[...].astype(F32), jnp.zeros((SLOT - OWN, PART), F32)], axis=0)
    f_out[...] = pltpu.roll(block, own_lead, 0).astype(BF16)
    f_in[...] = jnp.zeros_like(f_in)
    total_r[...] = jnp.zeros_like(total_r)

    barrier = pltpu.get_barrier_semaphore()
    cross = jnp.where(h == 0, before, after)
    peers = [(member(lax.rem(j + i, GROUP), z), x) for i in range(1, GROUP)]
    peers += [(at_place(y, z + 1, h), x), (at_place(y, z - 1, h), x), (cross, x)]
    peers += [(s, lax.rem(x + i, NX)) for i in range(1, NX)]
    mirror = at_place(x, z, 0)
    same_chip = x == y
    maybe = [(to_a, x, to_a != s), (to_b, x, own_two & (to_b != s)), (from_a, x, from_a != s), (from_b, x, my_two & (from_b != s)),
             (mirror + h, y, ~same_chip), (mirror + 1 - h, y, ~same_chip)]
    count = len(peers)
    for peer in peers:
        pl.semaphore_signal(barrier, inc=1, device_id=peer, device_id_type=MESH)
    for seq, section, when in maybe:
        count = count + when.astype(I32)

        @pl.when(when)
        def _(seq=seq, section=section):
            pl.semaphore_signal(barrier, inc=1, device_id=(seq, section), device_id_type=MESH)
    pl.semaphore_wait(barrier, count)

    send("pre_first", pre.at[pl.ds(0, EDGE)], halo_p.at[1], (before, x))
    send("pre_last", pre.at[pl.ds(ROWS - EDGE, EDGE)], halo_p.at[0], (after, x))
    send("emb_first", emb.at[pl.ds(0, EDGE)], halo_e.at[1], (before, x))
    send("emb_last", emb.at[pl.ds(ROWS // 2 - EDGE, EDGE)], halo_e.at[0], (after, x))
    send("filter_a", f_out, f_in.at[0], (to_a, x), to_a != s)
    send("filter_b", f_out, f_in.at[1], (to_b, x), own_two & (to_b != s))

    mine = pl.ds(pl.multiple_of(j * ROWS, ROWS), ROWS)
    row, lane = iota((QUARTER, 256), 0), iota((QUARTER, 256), 1)
    for i in range(GROUP):
        jj = lax.rem(j + i, GROUP)
        first = jj * CHUNK + x * QUARTER
        tile = jnp.minimum(first // 128, C_IN // 128 - 2)
        hit = (lane - row == first - tile * 128) & (row < CHUNK - x * QUARTER)
        seen = acts[:, pl.ds(pl.multiple_of(tile * 128, 128), 256)]
        piece = nt_dot(jnp.where(hit, 1.0, 0.0).astype(BF16), seen).astype(BF16)
        if i == 0:
            at[x, :, mine] = piece
        else:
            at_s[i - 1] = piece
            send(f"acts_{i}", at_s.at[i - 1], at.at[x, :, mine], (member(jj, z), x))

    for i, name in enumerate(("last", "first")):
        arrive("pre_" + name, halo_p.at[i])
        arrive("emb_" + name, halo_e.at[i])
    pick = (8 + iota((ROWS + 2 * EDGE, ROWS // 2 + 2 * EDGE), 0) // 2 == iota((ROWS + 2 * EDGE, ROWS // 2 + 2 * EDGE), 1)).astype(BF16)
    up = jnp.dot(pick, jnp.concatenate([halo_e[0], emb[...], halo_e[1]], axis=0), preferred_element_type=F32) * 0.5
    value = jnp.concatenate([halo_p[0], pre[...], halo_p[1]], axis=0).astype(F32)
    grad = up * gelu_slope(value)
    low = jnp.where(s > 0, 1.0, 0.0)
    high = jnp.where(s < SHARDS - 1, 1.0, 0.0)
    dzx[j, 0:EDGE] = jnp.concatenate([grad[8:16] * low, grad[ROWS + EDGE:ROWS + EDGE + 8] * high], axis=0).astype(BF16)
    dzx[j, EDGE:EDGE + ROWS] = grad[EDGE:EDGE + ROWS].astype(BF16)

    for i in (1, 3, 2):
        send(f"dz_{i}", dzx.at[j], dzx.at[j], (at_place(y + i, z, h), x))
    send("dz_sib_0", dzx.at[j], dzx.at[j], (sibling, x))

    def gather(t):
        if t == 0:
            arrive("filter_a", f_in.at[0], from_a != s)
            arrive("filter_b", f_in.at[1], my_two & (from_b != s))

            @pl.when(to_a == s)
            def _():
                f_in[0] = f_out[...]

            @pl.when(own_two & (to_b == s))
            def _():
                f_in[1] = f_out[...]

            f_slots[z] = jnp.where(iota((SLOT, PART), 0) < my_cut, f_in[0].astype(F32), f_in[1].astype(F32)).astype(BF16)
        for side, sign in ((0, 1), (1, -1)):
            if side == 1 and t == 4:
                continue
            slot = lax.rem(z - sign * t + NZ, NZ)
            if t > 0:
                arrive(f"gather_{side}_{t - 1}", f_slots.at[slot])
            if t < (4 if side == 0 else 3):
                send(f"gather_{side}_{t}", f_slots.at[slot], f_slots.at[slot], (at_place(y, z + sign, h), x))

    def shifts(b):
        edge = dzx[b, 0:EDGE].astype(F32)
        rim[8:16, :] = edge[0:8]
        rim[16:16 + ROWS, :] = dzx[b, EDGE:EDGE + ROWS].astype(F32)
        rim[16 + ROWS:24 + ROWS, :] = edge[8:16]
        place = pl.ds(pl.multiple_of(b * ROWS, ROWS), ROWS)
        for k in range(TAPS):
            dz[k, place, :] = rim[18 - k:18 - k + ROWS, :].astype(BF16)

    def from_y(i):
        b = 2 * lax.rem(y - i + NY, NY) + h
        arrive(f"dz_{i}", dzx.at[b])
        send(f"dz_sib_{i}", dzx.at[b], dzx.at[b], (sibling, x))
        shifts(b)

    def from_sibling(i):
        b = 2 * lax.rem(y - i + NY, NY) + 1 - h
        arrive(f"dz_sib_{i}", dzx.at[b])
        shifts(b)

    shifts(j)
    gather(0)
    for i in range(1, GROUP):
        b = lax.rem(j - i + GROUP, GROUP)
        arrive(f"acts_{i}", at.at[x, :, pl.ds(pl.multiple_of(b * ROWS, ROWS), ROWS)])
    for i in range(1, NX):
        send(f"acts_x_{i}", at.at[x], at.at[x], (s, lax.rem(x + i, NX)))
    from_sibling(0)
    gather(1)
    gather(2)
    from_y(1)
    from_y(3)
    gather(3)
    from_sibling(1)
    from_sibling(3)
    gather(4)
    from_y(2)
    from_sibling(2)
    for i in range(1, NX):
        arrive(f"acts_x_{i}", at.at[lax.rem(x - i + NX, NX)])

    part[SPACE:SPACE + 16, :] = jnp.zeros((16, PART), F32)
    columns = at[...].reshape(NX * QUARTER, GROUP * ROWS)
    for w in range(TAPS):
        rows = jnp.dot(columns, dz[tap_of(w)], preferred_element_type=F32)
        part[w * CHUNK:(w + 1) * CHUNK, :] = rows[0:CHUNK]

    HALF = SLOT // 2

    def reduce(t):
        for half in range(2):
            for side, sign in ((0, 1), (1, -1)):
                if t == 0 and side != half:
                    continue
                out, got = (s_r, g_r) if side == 0 else (s_l, g_l)
                dest = lax.rem(z + sign * (4 - t) + NZ, NZ)
                tile = (dest * OWN) // 16 * 16
                value = part[pl.ds(pl.multiple_of(tile + half * HALF, 16), HALF), :]
                if t > 0 and (t > 1 or side == half):
                    arrive(f"red_{side}_{t - 1}_{half}", got.at[t - 1, half])
                    value = value + got[t - 1, half].astype(F32)
                out[t, half] = value.astype(BF16)
                send(f"red_{side}_{t}_{half}", out.at[t, half], got.at[t, half], (at_place(y, z + sign, h), x))

    def reduce_end():
        for half in range(2):
            arrive(f"red_0_3_{half}", g_r.at[3, half])
            arrive(f"red_1_3_{half}", g_l.at[3, half])
            value = part[pl.ds(pl.multiple_of(my_tile + half * HALF, 16), HALF), :]
            value = value + g_r[3, half].astype(F32) + g_l[3, half].astype(F32)
            total_s[half * HALF:(half + 1) * HALF, :] = value.astype(BF16)
        send("total_a", total_s, total_r.at[0], (from_a, x), from_a != s)
        send("total_b", total_s, total_r.at[1], (from_b, x), my_two & (from_b != s))

    def pack():
        f_all[0:16, :] = jnp.zeros((16, PART), BF16)
        for u in range(NZ):
            base = u * OWN // 16 * 16
            f_all[base:base + 16, :] += f_slots[u, 0:16]
            f_all[base + 16:base + SLOT, :] = f_slots[u, 16:SLOT]

    def input_grad(i):
        dest = lax.rem(x + i, NX)
        for hh in range(2):
            place = pl.ds(pl.multiple_of((2 * dest + hh) * ROWS, ROWS), ROWS)
            total = jnp.zeros((CHUNK, ROWS), F32)
            for w in range(TAPS):
                total += nt_dot(f_all[w * CHUNK:(w + 1) * CHUNK, :], dz[tap_of(w), place, :])
            if i == 0:
                ig_own[:, hh * ROWS:(hh + 1) * ROWS] = total
            else:
                ig_s[i - 1, :, hh * ROWS:(hh + 1) * ROWS] = total.astype(BF16)
        if i > 0:
            send(f"ig_{i}", ig_s.at[i - 1], ig_r.at[i - 1], (s, dest))

    def input_grad_end():
        total = ig_own[...]
        for i in range(1, NX):
            arrive(f"ig_{i}", ig_r.at[i - 1])
            total += ig_r[i - 1].astype(F32)
        place = pl.ds(pl.multiple_of(h * CHUNK, 16), CHUNK)
        for hh in range(2):
            fin_s[hh] = total[:, hh * ROWS:(hh + 1) * ROWS].astype(BF16)
        other = 1 - h
        send("final_same", fin_s.at[h], ig_out.at[place], (mirror + h, y), ~same_chip)
        send("final_other", fin_s.at[other], ig_out.at[place], (jnp.where(same_chip, sibling, mirror + other), y))

        @pl.when(same_chip)
        def _():
            ig_out[place, :] = fin_s[h]

    reduce(0)
    pack()
    input_grad(1)
    reduce(1)
    input_grad(2)
    reduce(2)
    input_grad(3)
    reduce(3)
    input_grad(0)
    reduce_end()
    input_grad_end()

    arrive("total_a", total_r.at[0], to_a != s)
    arrive("total_b", total_r.at[1], own_two & (to_b != s))

    @pl.when(to_a == s)
    def _():
        total_r[0] = total_s[...]

    @pl.when(own_two & (to_b == s))
    def _():
        total_r[1] = total_s[...]

    rows = jnp.where(iota((SLOT, PART), 0) < own_cut, total_r[0].astype(F32), total_r[1].astype(F32))
    fg_out[...] = pltpu.roll(rows, lax.rem(SLOT - own_lead, SLOT), 0)[0:OWN] * scale

    arrive("final_same", ig_out.at[pl.ds(pl.multiple_of(h * CHUNK, 16), CHUNK)], ~same_chip)
    arrive("final_other", ig_out.at[pl.ds(pl.multiple_of((1 - h) * CHUNK, 16), CHUNK)])
    for copy, when in started:
        if when is None:
            copy.wait_send()
        else:
            pl.when(when)(copy.wait_send)


def shards(acts, pre_act, emb_grad, filters):
    total_rows = acts.shape[0] * lax.axis_size("seq")
    vmem = pl.BlockSpec(memory_space=pltpu.VMEM)
    across, filter_grad = pl.pallas_call(
        functools.partial(kernel, 1.0 / math.sqrt(total_rows)),
        out_shape=(jax.ShapeDtypeStruct((SLICE, ROWS), BF16), jax.ShapeDtypeStruct((OWN, PART), F32)),
        in_specs=[vmem] * 4,
        out_specs=(vmem, vmem),
        scratch_shapes=[
            pltpu.VMEM((SLOT, PART), BF16),
            pltpu.VMEM((2, SLOT, PART), BF16),
            pltpu.VMEM((NZ, SLOT, PART), BF16),
            pltpu.VMEM((SPACE + 16, PART), BF16),
            pltpu.VMEM((2, EDGE, PART), BF16),
            pltpu.VMEM((2, EDGE, PART), BF16),
            pltpu.VMEM((ROWS + 2 * EDGE, PART), F32),
            pltpu.VMEM((GROUP, ROWS + EDGE, PART), BF16),
            pltpu.VMEM((TAPS, GROUP * ROWS, PART), BF16),
            pltpu.VMEM((GROUP - 1, QUARTER, ROWS), BF16),
            pltpu.VMEM((NX, QUARTER, GROUP * ROWS), BF16),
            pltpu.VMEM((SPACE + 16, PART), F32),
            pltpu.VMEM((4, 2, SLOT // 2, PART), BF16),
            pltpu.VMEM((4, 2, SLOT // 2, PART), BF16),
            pltpu.VMEM((4, 2, SLOT // 2, PART), BF16),
            pltpu.VMEM((4, 2, SLOT // 2, PART), BF16),
            pltpu.VMEM((SLOT, PART), BF16),
            pltpu.VMEM((2, SLOT, PART), BF16),
            pltpu.VMEM((CHUNK, 2 * ROWS), F32),
            pltpu.VMEM((NX - 1, CHUNK, 2 * ROWS), BF16),
            pltpu.VMEM((NX - 1, CHUNK, 2 * ROWS), BF16),
            pltpu.VMEM((2, CHUNK, ROWS), BF16),
            pltpu.SemaphoreType.DMA((64,)),
            pltpu.SemaphoreType.DMA((64,)),
        ],
        compiler_params=pltpu.CompilerParams(collective_id=0, has_side_effects=True, vmem_limit_bytes=48 << 20),
    )(acts, pre_act, emb_grad, filters)
    return across.T, filter_grad


def solution(mesh):
    in_specs = (P("seq", None), P("seq", "section"), P("seq", "section"), P("seq", "section"))
    out_specs = (P("seq", "section"), P("seq", "section"))
    return jax.shard_map(shards, mesh=mesh, in_specs=in_specs, out_specs=out_specs, check_vma=False)
```

```python
import functools
import math

import jax
import jax.numpy as jnp
from jax import lax
from jax.experimental import pallas as pl
from jax.experimental.pallas import tpu as pltpu
from jax.sharding import PartitionSpec as P

MESH = pl.DeviceIdType.MESH
F32, BF16 = jnp.float32, jnp.bfloat16
I32 = jnp.int32
TAPS = 5
NX, NY, NZ = 4, 4, 8
GROUP = 8
SHARDS = 64
C_IN = 1408
ROWS = 256
PART = 384
OWN = 110
SLOT = 128
CHUNK = C_IN // GROUP
QUARTER = 48
SPACE = TAPS * CHUNK
SLICE = C_IN // NX
EDGE = 16


def gelu_slope(value):
    cumul = 0.5 * (1.0 + lax.erf(value * 0.7071067811865476))
    dens = jnp.exp(-0.5 * value * value) * 0.3989422804014327
    return cumul + value * dens


def nt_dot(a, b):
    return lax.dot_general(a, b, (((1,), (1,)), ((), ())), preferred_element_type=F32)


def iota(shape, axis):
    return lax.broadcasted_iota(I32, shape, axis)


def kernel(scale, acts_hbm, pre_hbm, emb_hbm, filt_hbm, ig_out, fg_out, acts, pre, emb, filt, f_out, f_in, f_slots, f_all, halo_p, halo_e, rim, dzx, dz, at_s, at, part,
           s_r, s_l, g_r, g_l, total_s, total_r, ig_own, ig_s, ig_r, fin_s, load_sem, send_sem, recv_sem):
    s = lax.axis_index("seq")
    x = lax.axis_index("section")
    y, z, h = s // 16, lax.rem(s, 16) // 2, lax.rem(s, 2)
    j = 2 * y + h

    def at_place(yy, zz, hh):
        return lax.rem(yy + NY, NY) * 16 + lax.rem(zz + NZ, NZ) * 2 + hh

    def member(jj, zz):
        return (jj // 2) * 16 + zz * 2 + lax.rem(jj, 2)

    sibling = s + 1 - 2 * h
    after = lax.rem(s + 1, SHARDS)
    before = lax.rem(s + SHARDS - 1, SHARDS)

    def row_block(u):
        tile = (u * OWN) // 16 * 16
        chunk = (u * OWN) // CHUNK
        cut = (chunk + 1) * CHUNK - tile
        lead = u * OWN - tile
        return tile, chunk, cut, lead, cut < lead + OWN

    own_v, own_u = s // 8, lax.rem(s, 8)
    _, own_w, own_cut, own_lead, own_two = row_block(own_u)
    to_a = member(lax.rem(5 * own_v + own_w, GROUP), own_u)
    to_b = member(lax.rem(5 * own_v + own_w + 1, GROUP), own_u)
    my_tile, my_w, my_cut, my_lead, my_two = row_block(z)

    def tap_of(w):
        return lax.rem(2 * w + 3 * j, TAPS)

    def owner_of(w):
        return (8 * tap_of(w) + j) // 5 * 8 + z

    from_a, from_b = owner_of(my_w), owner_of(my_w + 1)

    ids = {}
    started = []

    def sem(name):
        return ids.setdefault(name, len(ids))

    def describe(name, src, dst, to):
        i = sem(name)
        return pltpu.make_async_remote_copy(src_ref=src, dst_ref=dst, send_sem=send_sem.at[i], recv_sem=recv_sem.at[i],
                                            device_id=to, device_id_type=MESH)

    def send(name, src, dst, to, when=None):
        copy = describe(name, src, dst, to)
        started.append((copy, when))
        if when is None:
            copy.start()
        else:
            pl.when(when)(copy.start)

    def arrive(name, dst, when=None):
        copy = describe(name, dst, dst, (sibling, x))
        if when is None:
            copy.wait_recv()
        else:
            pl.when(when)(copy.wait_recv)

    loads = []
    for i, (src, dst) in enumerate(((filt_hbm, filt), (pre_hbm, pre), (emb_hbm, emb), (acts_hbm, acts))):
        loads.append(pltpu.make_async_copy(src, dst, load_sem.at[i]))
        loads[-1].start()
    loads[0].wait()

    block = jnp.concatenate([filt[...].astype(F32), jnp.zeros((SLOT - OWN, PART), F32)], axis=0)
    f_out[...] = pltpu.roll(block, own_lead, 0).astype(BF16)
    f_in[...] = jnp.zeros_like(f_in)
    total_r[...] = jnp.zeros_like(total_r)

    barrier = pltpu.get_barrier_semaphore()
    cross = jnp.where(h == 0, before, after)
    peers = [(member(lax.rem(j + i, GROUP), z), x) for i in range(1, GROUP)]
    peers += [(at_place(y, z + 1, h), x), (at_place(y, z - 1, h), x), (cross, x)]
    peers += [(s, lax.rem(x + i, NX)) for i in range(1, NX)]
    mirror = at_place(x, z, 0)
    same_chip = x == y
    maybe = [(to_a, x, to_a != s), (to_b, x, own_two & (to_b != s)), (from_a, x, from_a != s), (from_b, x, my_two & (from_b != s)),
             (mirror + h, y, ~same_chip), (mirror + 1 - h, y, ~same_chip)]
    count = len(peers)
    for peer in peers:
        pl.semaphore_signal(barrier, inc=1, device_id=peer, device_id_type=MESH)
    for seq, section, when in maybe:
        count = count + when.astype(I32)

        @pl.when(when)
        def _(seq=seq, section=section):
            pl.semaphore_signal(barrier, inc=1, device_id=(seq, section), device_id_type=MESH)
    for load in loads[1:]:
        load.wait()
    pl.semaphore_wait(barrier, count)

    send("pre_first", pre.at[pl.ds(0, EDGE)], halo_p.at[1], (before, x))
    send("pre_last", pre.at[pl.ds(ROWS - EDGE, EDGE)], halo_p.at[0], (after, x))
    send("emb_first", emb.at[pl.ds(0, EDGE)], halo_e.at[1], (before, x))
    send("emb_last", emb.at[pl.ds(ROWS // 2 - EDGE, EDGE)], halo_e.at[0], (after, x))
    send("filter_a", f_out, f_in.at[0], (to_a, x), to_a != s)
    send("filter_b", f_out, f_in.at[1], (to_b, x), own_two & (to_b != s))

    mine = pl.ds(pl.multiple_of(j * ROWS, ROWS), ROWS)
    row, lane = iota((QUARTER, 256), 0), iota((QUARTER, 256), 1)
    for i in range(GROUP):
        jj = lax.rem(j + i, GROUP)
        first = jj * CHUNK + x * QUARTER
        tile = jnp.minimum(first // 128, C_IN // 128 - 2)
        hit = (lane - row == first - tile * 128) & (row < CHUNK - x * QUARTER)
        seen = acts[:, pl.ds(pl.multiple_of(tile * 128, 128), 256)]
        piece = nt_dot(jnp.where(hit, 1.0, 0.0).astype(BF16), seen).astype(BF16)
        if i == 0:
            at[x, :, mine] = piece
        else:
            at_s[i - 1] = piece
            send(f"acts_{i}", at_s.at[i - 1], at.at[x, :, mine], (member(jj, z), x))

    for i, name in enumerate(("last", "first")):
        arrive("pre_" + name, halo_p.at[i])
        arrive("emb_" + name, halo_e.at[i])
    pick = (8 + iota((ROWS + 2 * EDGE, ROWS // 2 + 2 * EDGE), 0) // 2 == iota((ROWS + 2 * EDGE, ROWS // 2 + 2 * EDGE), 1)).astype(BF16)
    up = jnp.dot(pick, jnp.concatenate([halo_e[0], emb[...], halo_e[1]], axis=0), preferred_element_type=F32) * 0.5
    value = jnp.concatenate([halo_p[0], pre[...], halo_p[1]], axis=0).astype(F32)
    grad = up * gelu_slope(value)
    low = jnp.where(s > 0, 1.0, 0.0)
    high = jnp.where(s < SHARDS - 1, 1.0, 0.0)
    dzx[j, 0:EDGE] = jnp.concatenate([grad[8:16] * low, grad[ROWS + EDGE:ROWS + EDGE + 8] * high], axis=0).astype(BF16)
    dzx[j, EDGE:EDGE + ROWS] = grad[EDGE:EDGE + ROWS].astype(BF16)

    for i in (1, 3, 2):
        send(f"dz_{i}", dzx.at[j], dzx.at[j], (at_place(y + i, z, h), x))
    send("dz_sib_0", dzx.at[j], dzx.at[j], (sibling, x))

    def gather(t):
        if t == 0:
            arrive("filter_a", f_in.at[0], from_a != s)
            arrive("filter_b", f_in.at[1], my_two & (from_b != s))

            @pl.when(to_a == s)
            def _():
                f_in[0] = f_out[...]

            @pl.when(own_two & (to_b == s))
            def _():
                f_in[1] = f_out[...]

            f_slots[z] = jnp.where(iota((SLOT, PART), 0) < my_cut, f_in[0].astype(F32), f_in[1].astype(F32)).astype(BF16)
        for side, sign in ((0, 1), (1, -1)):
            if side == 1 and t == 4:
                continue
            slot = lax.rem(z - sign * t + NZ, NZ)
            if t > 0:
                arrive(f"gather_{side}_{t - 1}", f_slots.at[slot])
            if t < (4 if side == 0 else 3):
                send(f"gather_{side}_{t}", f_slots.at[slot], f_slots.at[slot], (at_place(y, z + sign, h), x))

    def shifts(b):
        edge = dzx[b, 0:EDGE].astype(F32)
        rim[8:16, :] = edge[0:8]
        rim[16:16 + ROWS, :] = dzx[b, EDGE:EDGE + ROWS].astype(F32)
        rim[16 + ROWS:24 + ROWS, :] = edge[8:16]
        place = pl.ds(pl.multiple_of(b * ROWS, ROWS), ROWS)
        for k in range(TAPS):
            dz[k, place, :] = rim[18 - k:18 - k + ROWS, :].astype(BF16)

    def from_y(i):
        b = 2 * lax.rem(y - i + NY, NY) + h
        arrive(f"dz_{i}", dzx.at[b])
        send(f"dz_sib_{i}", dzx.at[b], dzx.at[b], (sibling, x))
        shifts(b)

    def from_sibling(i):
        b = 2 * lax.rem(y - i + NY, NY) + 1 - h
        arrive(f"dz_sib_{i}", dzx.at[b])
        shifts(b)

    shifts(j)
    for i in range(1, GROUP):
        b = lax.rem(j - i + GROUP, GROUP)
        arrive(f"acts_{i}", at.at[x, :, pl.ds(pl.multiple_of(b * ROWS, ROWS), ROWS)])
    for i in range(1, NX):
        send(f"acts_x_{i}", at.at[x], at.at[x], (s, lax.rem(x + i, NX)))
    from_sibling(0)
    gather(0)
    from_y(1)
    from_y(3)
    gather(1)
    from_sibling(1)
    from_sibling(3)
    gather(2)
    from_y(2)
    from_sibling(2)
    for i in range(1, NX):
        arrive(f"acts_x_{i}", at.at[lax.rem(x - i + NX, NX)])

    part[SPACE:SPACE + 16, :] = jnp.zeros((16, PART), F32)
    columns = at[...].reshape(NX * QUARTER, GROUP * ROWS)
    for w in range(TAPS):
        rows = jnp.dot(columns, dz[tap_of(w)], preferred_element_type=F32)
        part[w * CHUNK:(w + 1) * CHUNK, :] = rows[0:CHUNK]

    HALF = SLOT // 2

    def reduce(t):
        for half in range(2):
            for side, sign in ((0, 1), (1, -1)):
                if t == 0 and side != half:
                    continue
                out, got = (s_r, g_r) if side == 0 else (s_l, g_l)
                dest = lax.rem(z + sign * (4 - t) + NZ, NZ)
                tile = (dest * OWN) // 16 * 16
                value = part[pl.ds(pl.multiple_of(tile + half * HALF, 16), HALF), :]
                if t > 0 and (t > 1 or side == half):
                    arrive(f"red_{side}_{t - 1}_{half}", got.at[t - 1, half])
                    value = value + got[t - 1, half].astype(F32)
                out[t, half] = value.astype(BF16)
                send(f"red_{side}_{t}_{half}", out.at[t, half], got.at[t, half], (at_place(y, z + sign, h), x))

    def reduce_end():
        for half in range(2):
            arrive(f"red_0_3_{half}", g_r.at[3, half])
            arrive(f"red_1_3_{half}", g_l.at[3, half])
            value = part[pl.ds(pl.multiple_of(my_tile + half * HALF, 16), HALF), :]
            value = value + g_r[3, half].astype(F32) + g_l[3, half].astype(F32)
            total_s[half * HALF:(half + 1) * HALF, :] = value.astype(BF16)
        send("total_a", total_s, total_r.at[0], (from_a, x), from_a != s)
        send("total_b", total_s, total_r.at[1], (from_b, x), my_two & (from_b != s))

    def pack():
        f_all[0:16, :] = jnp.zeros((16, PART), BF16)
        for u in range(NZ):
            base = u * OWN // 16 * 16
            f_all[base:base + 16, :] += f_slots[u, 0:16]
            f_all[base + 16:base + SLOT, :] = f_slots[u, 16:SLOT]

    def input_grad(i, hh):
        dest = lax.rem(x + i, NX)
        place = pl.ds(pl.multiple_of((2 * dest + hh) * ROWS, ROWS), ROWS)
        total = jnp.zeros((CHUNK, ROWS), F32)
        for w in range(TAPS):
            total += nt_dot(f_all[w * CHUNK:(w + 1) * CHUNK, :], dz[tap_of(w), place, :])
        if i == 0:
            ig_own[hh] = total
        else:
            ig_s[i - 1, hh] = total.astype(BF16)
            send(f"ig_{i}_{hh}", ig_s.at[i - 1, hh], ig_r.at[i - 1, hh], (s, dest))

    own_rows = pl.ds(pl.multiple_of(h * CHUNK, 16), CHUNK)
    other_rows = pl.ds(pl.multiple_of((1 - h) * CHUNK, 16), CHUNK)
    final_base = [sem("final_0"), sem("final_1")][0]

    def input_grad_end(hh):
        total = ig_own[hh]
        for i in range(1, NX):
            arrive(f"ig_{i}_{hh}", ig_r.at[i - 1, hh])
            total += ig_r[i - 1, hh].astype(F32)
        fin_s[hh] = total.astype(BF16)
        here = same_chip & (h == hh)
        copy = pltpu.make_async_remote_copy(src_ref=fin_s.at[hh], dst_ref=ig_out.at[own_rows], send_sem=send_sem.at[final_base + hh],
                                            recv_sem=recv_sem.at[final_base + lax.rem(h + hh, 2)], device_id=(mirror + hh, y),
                                            device_id_type=MESH)
        pl.when(~here)(copy.start)
        started.append((copy, ~here))

        @pl.when(here)
        def _():
            ig_out[own_rows, :] = fin_s[hh]

    gather(3)
    reduce(0)
    gather(4)
    pack()
    input_grad(1, 0)
    reduce(1)
    input_grad(2, 0)
    input_grad(3, 0)
    reduce(2)
    input_grad(0, 0)
    input_grad(1, 1)
    input_grad(2, 1)
    reduce(3)
    input_grad(3, 1)
    input_grad(0, 1)
    input_grad_end(0)
    reduce_end()
    input_grad_end(1)

    arrive("total_a", total_r.at[0], to_a != s)
    arrive("total_b", total_r.at[1], own_two & (to_b != s))

    @pl.when(to_a == s)
    def _():
        total_r[0] = total_s[...]

    @pl.when(own_two & (to_b == s))
    def _():
        total_r[1] = total_s[...]

    rows = jnp.where(iota((SLOT, PART), 0) < own_cut, total_r[0].astype(F32), total_r[1].astype(F32))
    fg_out[...] = pltpu.roll(rows, lax.rem(SLOT - own_lead, SLOT), 0)[0:OWN] * scale

    arrive("final_0", ig_out.at[own_rows], ~same_chip)
    arrive("final_1", ig_out.at[other_rows])
    for copy, when in started:
        if when is None:
            copy.wait_send()
        else:
            pl.when(when)(copy.wait_send)


def shards(acts, pre_act, emb_grad, filters):
    total_rows = acts.shape[0] * lax.axis_size("seq")
    vmem = pl.BlockSpec(memory_space=pltpu.VMEM)
    across, filter_grad = pl.pallas_call(
        functools.partial(kernel, 1.0 / math.sqrt(total_rows)),
        out_shape=(jax.ShapeDtypeStruct((SLICE, ROWS), BF16), jax.ShapeDtypeStruct((OWN, PART), F32)),
        in_specs=[pl.BlockSpec(memory_space=pl.ANY)] * 4,
        out_specs=(vmem, vmem),
        scratch_shapes=[
            pltpu.VMEM((ROWS, C_IN), BF16),
            pltpu.VMEM((ROWS, PART), BF16),
            pltpu.VMEM((ROWS // 2, PART), BF16),
            pltpu.VMEM((OWN, PART), BF16),
            pltpu.VMEM((SLOT, PART), BF16),
            pltpu.VMEM((2, SLOT, PART), BF16),
            pltpu.VMEM((NZ, SLOT, PART), BF16),
            pltpu.VMEM((SPACE + 16, PART), BF16),
            pltpu.VMEM((2, EDGE, PART), BF16),
            pltpu.VMEM((2, EDGE, PART), BF16),
            pltpu.VMEM((ROWS + 2 * EDGE, PART), F32),
            pltpu.VMEM((GROUP, ROWS + EDGE, PART), BF16),
            pltpu.VMEM((TAPS, GROUP * ROWS, PART), BF16),
            pltpu.VMEM((GROUP - 1, QUARTER, ROWS), BF16),
            pltpu.VMEM((NX, QUARTER, GROUP * ROWS), BF16),
            pltpu.VMEM((SPACE + 16, PART), F32),
            pltpu.VMEM((4, 2, SLOT // 2, PART), BF16),
            pltpu.VMEM((4, 2, SLOT // 2, PART), BF16),
            pltpu.VMEM((4, 2, SLOT // 2, PART), BF16),
            pltpu.VMEM((4, 2, SLOT // 2, PART), BF16),
            pltpu.VMEM((SLOT, PART), BF16),
            pltpu.VMEM((2, SLOT, PART), BF16),
            pltpu.VMEM((2, CHUNK, ROWS), F32),
            pltpu.VMEM((NX - 1, 2, CHUNK, ROWS), BF16),
            pltpu.VMEM((NX - 1, 2, CHUNK, ROWS), BF16),
            pltpu.VMEM((2, CHUNK, ROWS), BF16),
            pltpu.SemaphoreType.DMA((4,)),
            pltpu.SemaphoreType.DMA((64,)),
            pltpu.SemaphoreType.DMA((64,)),
        ],
        compiler_params=pltpu.CompilerParams(collective_id=0, has_side_effects=True, vmem_limit_bytes=58 << 20),
    )(acts, pre_act, emb_grad, filters)
    return across.T, filter_grad


def solution(mesh):
    in_specs = (P("seq", None), P("seq", "section"), P("seq", "section"), P("seq", "section"))
    out_specs = (P("seq", "section"), P("seq", "section"))
    return jax.shard_map(shards, mesh=mesh, in_specs=in_specs, out_specs=out_specs, check_vma=False)
```

```python
import functools
import math

import jax
import jax.numpy as jnp
from jax import lax
from jax.experimental import pallas as pl
from jax.experimental.pallas import tpu as pltpu
from jax.sharding import PartitionSpec as P

MESH = pl.DeviceIdType.MESH
F32, BF16 = jnp.float32, jnp.bfloat16
I32 = jnp.int32
TAPS = 5
NX, NY, NZ = 4, 4, 8
GROUP = 8
SHARDS = 64
C_IN = 1408
ROWS = 256
PART = 384
OWN = 110
SLOT = 128
CHUNK = C_IN // GROUP
QUARTER = 48
SPACE = TAPS * CHUNK
SLICE = C_IN // NX
EDGE = 16


def gelu_slope(value):
    cumul = 0.5 * (1.0 + lax.erf(value * 0.7071067811865476))
    dens = jnp.exp(-0.5 * value * value) * 0.3989422804014327
    return cumul + value * dens


def nt_dot(a, b):
    return lax.dot_general(a, b, (((1,), (1,)), ((), ())), preferred_element_type=F32)


def iota(shape, axis):
    return lax.broadcasted_iota(I32, shape, axis)


def kernel(scale, acts_hbm, pre_hbm, emb_hbm, filt_hbm, ig_out, fg_out, acts, pre, emb, filt, f_out, f_in, f_slots, f_all, halo_p, halo_e, rim, dzx, dz, at_s, at, part,
           s_r, s_l, g_r, g_l, total_s, total_r, ig_own, ig_s, ig_r, fin_s, load_sem, send_sem, recv_sem):
    s = lax.axis_index("seq")
    x = lax.axis_index("section")
    y, z, h = s // 16, lax.rem(s, 16) // 2, lax.rem(s, 2)
    j = 2 * y + h

    def at_place(yy, zz, hh):
        return lax.rem(yy + NY, NY) * 16 + lax.rem(zz + NZ, NZ) * 2 + hh

    def member(jj, zz):
        return (jj // 2) * 16 + zz * 2 + lax.rem(jj, 2)

    sibling = s + 1 - 2 * h
    after = lax.rem(s + 1, SHARDS)
    before = lax.rem(s + SHARDS - 1, SHARDS)

    def row_block(u):
        tile = (u * OWN) // 16 * 16
        chunk = (u * OWN) // CHUNK
        cut = (chunk + 1) * CHUNK - tile
        lead = u * OWN - tile
        return tile, chunk, cut, lead, cut < lead + OWN

    own_v, own_u = s // 8, lax.rem(s, 8)
    _, own_w, own_cut, own_lead, own_two = row_block(own_u)
    to_a = member(lax.rem(5 * own_v + own_w, GROUP), own_u)
    to_b = member(lax.rem(5 * own_v + own_w + 1, GROUP), own_u)
    my_tile, my_w, my_cut, my_lead, my_two = row_block(z)

    def tap_of(w):
        return lax.rem(2 * w + 3 * j, TAPS)

    def owner_of(w):
        return (8 * tap_of(w) + j) // 5 * 8 + z

    from_a, from_b = owner_of(my_w), owner_of(my_w + 1)

    ids = {}
    started = []

    def sem(name):
        return ids.setdefault(name, len(ids))

    def describe(name, src, dst, to):
        i = sem(name)
        return pltpu.make_async_remote_copy(src_ref=src, dst_ref=dst, send_sem=send_sem.at[i], recv_sem=recv_sem.at[i],
                                            device_id=to, device_id_type=MESH)

    def send(name, src, dst, to, when=None):
        copy = describe(name, src, dst, to)
        started.append((copy, when))
        if when is None:
            copy.start()
        else:
            pl.when(when)(copy.start)

    def arrive(name, dst, when=None):
        copy = describe(name, dst, dst, (sibling, x))
        if when is None:
            copy.wait_recv()
        else:
            pl.when(when)(copy.wait_recv)

    loads = []
    for i, (src, dst) in enumerate(((filt_hbm, filt), (pre_hbm, pre), (emb_hbm, emb), (acts_hbm, acts))):
        loads.append(pltpu.make_async_copy(src, dst, load_sem.at[i]))
        loads[-1].start()
    loads[0].wait()

    block = jnp.concatenate([filt[...].astype(F32), jnp.zeros((SLOT - OWN, PART), F32)], axis=0)
    f_out[...] = pltpu.roll(block, own_lead, 0).astype(BF16)
    f_in[...] = jnp.zeros_like(f_in)
    total_r[...] = jnp.zeros_like(total_r)

    barrier = pltpu.get_barrier_semaphore()
    cross = jnp.where(h == 0, before, after)
    peers = [(member(lax.rem(j + i, GROUP), z), x) for i in range(1, GROUP)]
    peers += [(at_place(y, z + 1, h), x), (at_place(y, z - 1, h), x), (cross, x)]
    peers += [(s, lax.rem(x + i, NX)) for i in range(1, NX)]
    mirror = at_place(x, z, 0)
    same_chip = x == y
    maybe = [(to_a, x, to_a != s), (to_b, x, own_two & (to_b != s)), (from_a, x, from_a != s), (from_b, x, my_two & (from_b != s)),
             (mirror + h, y, ~same_chip), (mirror + 1 - h, y, ~same_chip)]
    count = len(peers)
    for peer in peers:
        pl.semaphore_signal(barrier, inc=1, device_id=peer, device_id_type=MESH)
    for seq, section, when in maybe:
        count = count + when.astype(I32)

        @pl.when(when)
        def _(seq=seq, section=section):
            pl.semaphore_signal(barrier, inc=1, device_id=(seq, section), device_id_type=MESH)
    for load in loads[1:]:
        load.wait()
    pl.semaphore_wait(barrier, count)

    send("pre_first", pre.at[pl.ds(0, EDGE)], halo_p.at[1], (before, x))
    send("pre_last", pre.at[pl.ds(ROWS - EDGE, EDGE)], halo_p.at[0], (after, x))
    send("emb_first", emb.at[pl.ds(0, EDGE)], halo_e.at[1], (before, x))
    send("emb_last", emb.at[pl.ds(ROWS // 2 - EDGE, EDGE)], halo_e.at[0], (after, x))
    send("filter_a", f_out, f_in.at[0], (to_a, x), to_a != s)
    send("filter_b", f_out, f_in.at[1], (to_b, x), own_two & (to_b != s))

    mine = pl.ds(pl.multiple_of(j * ROWS, ROWS), ROWS)
    row, lane = iota((QUARTER, 256), 0), iota((QUARTER, 256), 1)
    for i in range(GROUP):
        jj = lax.rem(j + i, GROUP)
        first = jj * CHUNK + x * QUARTER
        tile = jnp.minimum(first // 128, C_IN // 128 - 2)
        hit = (lane - row == first - tile * 128) & (row < CHUNK - x * QUARTER)
        seen = acts[:, pl.ds(pl.multiple_of(tile * 128, 128), 256)]
        piece = nt_dot(jnp.where(hit, 1.0, 0.0).astype(BF16), seen).astype(BF16)
        if i == 0:
            at[x, :, mine] = piece
        else:
            at_s[i - 1] = piece
            send(f"acts_{i}", at_s.at[i - 1], at.at[x, :, mine], (member(jj, z), x))

    for i, name in enumerate(("last", "first")):
        arrive("pre_" + name, halo_p.at[i])
        arrive("emb_" + name, halo_e.at[i])
    pick = (8 + iota((ROWS + 2 * EDGE, ROWS // 2 + 2 * EDGE), 0) // 2 == iota((ROWS + 2 * EDGE, ROWS // 2 + 2 * EDGE), 1)).astype(BF16)
    up = jnp.dot(pick, jnp.concatenate([halo_e[0], emb[...], halo_e[1]], axis=0), preferred_element_type=F32) * 0.5
    value = jnp.concatenate([halo_p[0], pre[...], halo_p[1]], axis=0).astype(F32)
    grad = up * gelu_slope(value)
    low = jnp.where(s > 0, 1.0, 0.0)
    high = jnp.where(s < SHARDS - 1, 1.0, 0.0)
    dzx[j, 0:EDGE] = jnp.concatenate([grad[8:16] * low, grad[ROWS + EDGE:ROWS + EDGE + 8] * high], axis=0).astype(BF16)
    dzx[j, EDGE:EDGE + ROWS] = grad[EDGE:EDGE + ROWS].astype(BF16)

    for i in (1, 3, 2):
        send(f"dz_{i}", dzx.at[j], dzx.at[j], (at_place(y + i, z, h), x))
    send("dz_sib_0", dzx.at[j], dzx.at[j], (sibling, x))

    def gather(t):
        if t == 0:
            arrive("filter_a", f_in.at[0], from_a != s)
            arrive("filter_b", f_in.at[1], my_two & (from_b != s))

            @pl.when(to_a == s)
            def _():
                f_in[0] = f_out[...]

            @pl.when(own_two & (to_b == s))
            def _():
                f_in[1] = f_out[...]

            f_slots[z] = jnp.where(iota((SLOT, PART), 0) < my_cut, f_in[0].astype(F32), f_in[1].astype(F32)).astype(BF16)
        for side, sign in ((0, 1), (1, -1)):
            if side == 1 and t == 4:
                continue
            slot = lax.rem(z - sign * t + NZ, NZ)
            if t > 0:
                arrive(f"gather_{side}_{t - 1}", f_slots.at[slot])
            if t < (4 if side == 0 else 3):
                send(f"gather_{side}_{t}", f_slots.at[slot], f_slots.at[slot], (at_place(y, z + sign, h), x))

    def shifts(b):
        edge = dzx[b, 0:EDGE].astype(F32)
        rim[8:16, :] = edge[0:8]
        rim[16:16 + ROWS, :] = dzx[b, EDGE:EDGE + ROWS].astype(F32)
        rim[16 + ROWS:24 + ROWS, :] = edge[8:16]
        place = pl.ds(pl.multiple_of(b * ROWS, ROWS), ROWS)
        for k in range(TAPS):
            dz[k, place, :] = rim[18 - k:18 - k + ROWS, :].astype(BF16)

    def from_y(i):
        b = 2 * lax.rem(y - i + NY, NY) + h
        arrive(f"dz_{i}", dzx.at[b])
        send(f"dz_sib_{i}", dzx.at[b], dzx.at[b], (sibling, x))
        shifts(b)

    def from_sibling(i):
        b = 2 * lax.rem(y - i + NY, NY) + 1 - h
        arrive(f"dz_sib_{i}", dzx.at[b])
        shifts(b)

    shifts(j)
    from_sibling(0)
    gather(0)
    for i in range(1, GROUP):
        b = lax.rem(j - i + GROUP, GROUP)
        arrive(f"acts_{i}", at.at[x, :, pl.ds(pl.multiple_of(b * ROWS, ROWS), ROWS)])
    for i in range(1, NX):
        send(f"acts_x_{i}", at.at[x], at.at[x], (s, lax.rem(x + i, NX)))
    gather(1)
    from_y(1)
    from_y(3)
    from_sibling(1)
    from_sibling(3)
    gather(2)
    from_y(2)
    from_sibling(2)
    for i in range(1, NX):
        arrive(f"acts_x_{i}", at.at[lax.rem(x - i + NX, NX)])

    part[SPACE:SPACE + 16, :] = jnp.zeros((16, PART), F32)
    columns = at[...].reshape(NX * QUARTER, GROUP * ROWS)
    for w in range(TAPS):
        rows = jnp.dot(columns, dz[tap_of(w)], preferred_element_type=F32)
        part[w * CHUNK:(w + 1) * CHUNK, :] = rows[0:CHUNK]

    HALF = SLOT // 2

    def reduce(t):
        for half in range(2):
            for side, sign in ((0, 1), (1, -1)):
                if t == 0 and side != half:
                    continue
                out, got = (s_r, g_r) if side == 0 else (s_l, g_l)
                dest = lax.rem(z + sign * (4 - t) + NZ, NZ)
                tile = (dest * OWN) // 16 * 16
                value = part[pl.ds(pl.multiple_of(tile + half * HALF, 16), HALF), :]
                if t > 0 and (t > 1 or side == half):
                    arrive(f"red_{side}_{t - 1}_{half}", got.at[t - 1, half])
                    value = value + got[t - 1, half].astype(F32)
                out[t, half] = value.astype(BF16)
                send(f"red_{side}_{t}_{half}", out.at[t, half], got.at[t, half], (at_place(y, z + sign, h), x))

    def reduce_end():
        for half in range(2):
            arrive(f"red_0_3_{half}", g_r.at[3, half])
            arrive(f"red_1_3_{half}", g_l.at[3, half])
            value = part[pl.ds(pl.multiple_of(my_tile + half * HALF, 16), HALF), :]
            value = value + g_r[3, half].astype(F32) + g_l[3, half].astype(F32)
            total_s[half * HALF:(half + 1) * HALF, :] = value.astype(BF16)
        send("total_a", total_s, total_r.at[0], (from_a, x), from_a != s)
        send("total_b", total_s, total_r.at[1], (from_b, x), my_two & (from_b != s))

    def pack():
        f_all[0:16, :] = jnp.zeros((16, PART), BF16)
        for u in range(NZ):
            base = u * OWN // 16 * 16
            f_all[base:base + 16, :] += f_slots[u, 0:16]
            f_all[base + 16:base + SLOT, :] = f_slots[u, 16:SLOT]

    def input_grad(i, hh):
        dest = lax.rem(x + i, NX)
        place = pl.ds(pl.multiple_of((2 * dest + hh) * ROWS, ROWS), ROWS)
        total = jnp.zeros((CHUNK, ROWS), F32)
        for w in range(TAPS):
            total += nt_dot(f_all[w * CHUNK:(w + 1) * CHUNK, :], dz[tap_of(w), place, :])
        if i == 0:
            ig_own[hh] = total
        else:
            ig_s[i - 1, hh] = total.astype(BF16)
            send(f"ig_{i}_{hh}", ig_s.at[i - 1, hh], ig_r.at[i - 1, hh], (s, dest))

    own_rows = pl.ds(pl.multiple_of(h * CHUNK, 16), CHUNK)
    other_rows = pl.ds(pl.multiple_of((1 - h) * CHUNK, 16), CHUNK)
    final_base = [sem("final_0"), sem("final_1")][0]

    def input_grad_end(hh):
        total = ig_own[hh]
        for i in range(1, NX):
            arrive(f"ig_{i}_{hh}", ig_r.at[i - 1, hh])
            total += ig_r[i - 1, hh].astype(F32)
        fin_s[hh] = total.astype(BF16)
        here = same_chip & (h == hh)
        copy = pltpu.make_async_remote_copy(src_ref=fin_s.at[hh], dst_ref=ig_out.at[own_rows], send_sem=send_sem.at[final_base + hh],
                                            recv_sem=recv_sem.at[final_base + lax.rem(h + hh, 2)], device_id=(mirror + hh, y),
                                            device_id_type=MESH)
        pl.when(~here)(copy.start)
        started.append((copy, ~here))

        @pl.when(here)
        def _():
            ig_out[own_rows, :] = fin_s[hh]

    reduce(0)
    gather(3)
    gather(4)
    pack()
    input_grad(1, 0)
    reduce(1)
    input_grad(2, 0)
    input_grad(3, 0)
    reduce(2)
    input_grad(0, 0)
    input_grad(1, 1)
    input_grad(2, 1)
    reduce(3)
    input_grad(3, 1)
    input_grad(0, 1)
    input_grad_end(0)
    reduce_end()
    input_grad_end(1)

    arrive("total_a", total_r.at[0], to_a != s)
    arrive("total_b", total_r.at[1], own_two & (to_b != s))

    @pl.when(to_a == s)
    def _():
        total_r[0] = total_s[...]

    @pl.when(own_two & (to_b == s))
    def _():
        total_r[1] = total_s[...]

    rows = jnp.where(iota((SLOT, PART), 0) < own_cut, total_r[0].astype(F32), total_r[1].astype(F32))
    fg_out[...] = pltpu.roll(rows, lax.rem(SLOT - own_lead, SLOT), 0)[0:OWN] * scale

    arrive("final_0", ig_out.at[own_rows], ~same_chip)
    arrive("final_1", ig_out.at[other_rows])
    for copy, when in started:
        if when is None:
            copy.wait_send()
        else:
            pl.when(when)(copy.wait_send)


def shards(acts, pre_act, emb_grad, filters):
    total_rows = acts.shape[0] * lax.axis_size("seq")
    vmem = pl.BlockSpec(memory_space=pltpu.VMEM)
    across, filter_grad = pl.pallas_call(
        functools.partial(kernel, 1.0 / math.sqrt(total_rows)),
        out_shape=(jax.ShapeDtypeStruct((SLICE, ROWS), BF16), jax.ShapeDtypeStruct((OWN, PART), F32)),
        in_specs=[pl.BlockSpec(memory_space=pl.ANY)] * 4,
        out_specs=(vmem, vmem),
        scratch_shapes=[
            pltpu.VMEM((ROWS, C_IN), BF16),
            pltpu.VMEM((ROWS, PART), BF16),
            pltpu.VMEM((ROWS // 2, PART), BF16),
            pltpu.VMEM((OWN, PART), BF16),
            pltpu.VMEM((SLOT, PART), BF16),
            pltpu.VMEM((2, SLOT, PART), BF16),
            pltpu.VMEM((NZ, SLOT, PART), BF16),
            pltpu.VMEM((SPACE + 16, PART), BF16),
            pltpu.VMEM((2, EDGE, PART), BF16),
            pltpu.VMEM((2, EDGE, PART), BF16),
            pltpu.VMEM((ROWS + 2 * EDGE, PART), F32),
            pltpu.VMEM((GROUP, ROWS + EDGE, PART), BF16),
            pltpu.VMEM((TAPS, GROUP * ROWS, PART), BF16),
            pltpu.VMEM((GROUP - 1, QUARTER, ROWS), BF16),
            pltpu.VMEM((NX, QUARTER, GROUP * ROWS), BF16),
            pltpu.VMEM((SPACE + 16, PART), F32),
            pltpu.VMEM((4, 2, SLOT // 2, PART), BF16),
            pltpu.VMEM((4, 2, SLOT // 2, PART), BF16),
            pltpu.VMEM((4, 2, SLOT // 2, PART), BF16),
            pltpu.VMEM((4, 2, SLOT // 2, PART), BF16),
            pltpu.VMEM((SLOT, PART), BF16),
            pltpu.VMEM((2, SLOT, PART), BF16),
            pltpu.VMEM((2, CHUNK, ROWS), F32),
            pltpu.VMEM((NX - 1, 2, CHUNK, ROWS), BF16),
            pltpu.VMEM((NX - 1, 2, CHUNK, ROWS), BF16),
            pltpu.VMEM((2, CHUNK, ROWS), BF16),
            pltpu.SemaphoreType.DMA((4,)),
            pltpu.SemaphoreType.DMA((64,)),
            pltpu.SemaphoreType.DMA((64,)),
        ],
        compiler_params=pltpu.CompilerParams(collective_id=0, has_side_effects=True, vmem_limit_bytes=58 << 20),
    )(acts, pre_act, emb_grad, filters)
    return across.T, filter_grad


def solution(mesh):
    in_specs = (P("seq", None), P("seq", "section"), P("seq", "section"), P("seq", "section"))
    out_specs = (P("seq", "section"), P("seq", "section"))
    return jax.shard_map(shards, mesh=mesh, in_specs=in_specs, out_specs=out_specs, check_vma=False)
```
